1024 devices in a mesh: rep: 4 (over z_hi), fsdp: 256 (over z_lo, y, x, core).
Axes of the slice: x: 4, y: 4, z: 32 (z_hi: 4, z_lo: 8; z = z_hi * 8 + z_lo), core: 2. Of those that a mesh axis runs over, the one named last changes fastest.
Arguments:
- hidden: bfloat16 [262144, 4096], P(('rep', 'fsdp')), may hold values from -6 to 6
- weight: bfloat16 [512, 4096], P('fsdp'), may hold values from -0.09375 to 0.09375
- adapter_a: float32 [4096, 128], P('fsdp'), may hold values from -0.09375 to 0.09375
- adapter_b: float32 [512, 128], P('fsdp'), may hold values from -0.25 to 0.25
- grad_a: float32 [4, 4096, 128], P('rep', 'fsdp'), may hold values from -0.09375 to 0.09375
- grad_b: float32 [4, 512, 128], P('rep', 'fsdp'), may hold values from -0.25 to 0.25
Outputs:
- projected: bfloat16 [262144, 512], P(('rep', 'fsdp'))
- merged: bfloat16 [512, 4096], P('fsdp')
The draws below stay inside these ranges and needn't reach their ends.
All inputs are finite; a program needn't handle non-finite values.
Results may differ from the reference program's by a relative error of at most 0.0049.
Values may be sent and summed in bfloat16 or wider, within the bound.
A program may use at most 64 MiB of HBM per device.

```python
import jax
import jax.numpy as jnp
from jax import lax

IN = 4096
OUT = 512
RANK = 128
TOKENS = 262144
N_REP = 4


def levels(stream_key, shape, shards, smallest, largest):
    factor_of, own = 1.0, jax.random.fold_in(stream_key, 6)
    for axis_at, parts in shards:
        steps = jnp.exp(jax.random.uniform(jax.random.fold_in(own, axis_at), (parts,), jnp.float32, smallest / len(shards), largest / len(shards)))
        factor_of = factor_of * jnp.repeat(steps, shape[axis_at] // parts).reshape([-1 if axis == axis_at else 1 for axis in range(len(shape))])
    return factor_of


def centred(rng, extent, spread, bound, shards=(), dtype=jnp.bfloat16):
    values = spread * jax.random.normal(rng, extent, jnp.float32)
    if shards:
        values = values * levels(rng, extent, shards, -0.22, 0.18)
    return jnp.clip(values, -bound, bound).astype(dtype)


def setup_inputs(seed: int = 0) -> dict:
    key_list = jax.random.split(jax.random.key(seed), 7)
    return {
        "hidden": centred(key_list[0], (TOKENS, IN), 1.0, 6.0, ((0, 1024),)),
        "weight": centred(key_list[1], (OUT, IN), IN ** -0.5, 0.09375, ((0, 256),)),
        "adapter_a": centred(key_list[2], (IN, RANK), IN ** -0.5, 0.09375, ((0, 256),), jnp.float32),
        "adapter_b": centred(key_list[3], (OUT, RANK), 0.045, 0.25, ((0, 256),), jnp.float32),
        "grad_a": centred(key_list[4], (N_REP, IN, RANK), 0.0156, 0.09375, ((0, 4), (1, 256)), jnp.float32),
        "grad_b": centred(key_list[5], (N_REP, OUT, RANK), 0.045, 0.25, ((0, 4), (1, 256)), jnp.float32),
    }


step_size = 0.5


def reference(hidden, weight, adapter_a, adapter_b, grad_a, grad_b):
    mean_a = jnp.sum(grad_a, axis=0) / N_REP
    mean_b = jnp.sum(grad_b, axis=0) / N_REP
    new_a = adapter_a - step_size * mean_a
    new_b = adapter_b - step_size * mean_b
    delta = lax.dot_general(new_b, new_a, (((1,), (1,)), ((), ())), precision=lax.Precision.HIGHEST, preferred_element_type=jnp.float32)
    merged = (weight.astype(jnp.float32) + delta).astype(jnp.bfloat16)
    projected = lax.dot_general(hidden, merged, (((1,), (1,)), ((), ())), preferred_element_type=jnp.float32)
    return projected.astype(jnp.bfloat16), merged
```

```python
import jax
import jax.numpy as jnp
from jax import lax
from jax.experimental import pallas as pl
from jax.experimental.pallas import tpu as pltpu
from jax.sharding import Mesh
from jax.sharding import PartitionSpec as P

FSDP = ("fsdp_0", "fsdp_1", "fsdp_2", "fsdp_3")
REP_FSDP = ("rep", "fsdp_0", "fsdp_1", "fsdp_2", "fsdp_3")
MESH = pl.DeviceIdType.MESH
bf16, f32 = jnp.bfloat16, jnp.float32
NT = (((1,), (1,)), ((), ()))
step_size = 0.5


def split(v):
    hi = v.astype(bf16)
    return hi, (v - hi.astype(f32)).astype(bf16)


def dot_nt(a, b):
    return lax.dot_general(a, b, NT, preferred_element_type=f32)


def kernel(
    hid, wt, aa, ab, ga, gb, out, mrg,
    H, W, Pb, Pin, U, Uin, A, B, Bh, Bl, aav, abv, gav, gbv, Gr, Gbr, na, nb, nbp, BL, D, Din, wv,
    s_loc, s_own, s_g, r_g, s_g2, r_g2, s_wz, r_wz, s_wf, r_w, s_ws, s_w2, r_w2,
    s_az, r_az, s_bz, r_bz, s_af, s_as, r_a, s_bf, s_bs, r_b, s_d2d, r_d2d,
):
    r, z, y, x, c = (lax.axis_index(n) for n in REP_FSDP)
    gz = r * 8 + z
    zh, zs = lax.div(z, 4), lax.rem(z, 4)
    oc = 1 - c

    def dev(dz=0, dy=0, dx=0, core=c):
        g = lax.rem(gz + (dz + 32), 32)
        return (lax.div(g, 8), lax.rem(g, 8), lax.rem(y + dy, 4), lax.rem(x + dx, 4), core)

    F = [dev(dy=k * c, dx=k * oc) for k in range(4)]
    S = [dev(dy=k * oc, dx=k * c) for k in range(4)]
    partner = dev(core=oc)
    up, down = dev(dz=8), dev(dz=-8)
    far = 4 - 8 * c
    near = [dict(dz=d) for d in (1, -1, 2, -2, 3, -3)]
    zpeers = [dev(**n) for n in near] + [dev(dz=far)]
    zpairs = [(p[:4] + (0,), p[:4] + (1,)) for p in zpeers]
    opposite = dev(dz=-far)

    def at_f(k, s=0):
        return (
            lax.rem(y + (k * c + s * oc), 4),
            lax.rem(x + (k * oc + s * c), 4),
        )

    pending = []

    def send(src, dst, ss, rs, to):
        d = pltpu.make_async_remote_copy(
            src_ref=src, dst_ref=dst, send_sem=ss, recv_sem=rs, device_id=to, device_id_type=MESH
        )
        d.start()
        pending.append(d)

    def arrive(dst, rs):
        pltpu.make_async_copy(dst, dst, rs).wait()

    mine = pl.ds(pl.multiple_of(c * 2048, 2048), 2048)
    other = pl.ds(pl.multiple_of(oc * 2048, 2048), 2048)
    rows2 = pl.ds(4 * x + 2 * c, 2)
    loads = [
        pltpu.make_async_copy(ga.at[0], gav, s_loc.at[0]),
        pltpu.make_async_copy(gb.at[0], gbv, s_loc.at[1]),
        pltpu.make_async_copy(aa, aav, s_loc.at[2]),
        pltpu.make_async_copy(ab, abv, s_loc.at[3]),
        pltpu.make_async_copy(wt, wv, s_loc.at[4]),
        pltpu.make_async_copy(hid.at[:, mine], H.at[c], s_loc.at[5]),
    ]
    for l in loads:
        l.start()
    pltpu.make_async_copy(wt.at[:, mine], W.at[z, y, rows2, :], r_wz.at[z, c]).start()

    barrier = pltpu.get_barrier_semaphore()
    peers = [partner, up, down] + F[1:] + S[1:]
    for pair in zpairs + [(opposite[:4] + (0,), opposite[:4] + (1,))]:
        peers += list(pair)
    for p in peers:
        pl.semaphore_signal(barrier, inc=1, device_id=p, device_id_type=MESH)
    pl.semaphore_wait(barrier, len(peers))

    for i, to in enumerate((up, down)):
        send(ga.at[0], Gr.at[i], s_g.at[0, i], r_g.at[0, i], to)
        send(gb.at[0], Gbr.at[i], s_g.at[1, i], r_g.at[1, i], to)
    for j, pair in enumerate(zpairs):
        for h in range(2):
            send(wt.at[:, h * 2048 : h * 2048 + 2048], W.at[z, y, rows2, :], s_wz.at[j, h], r_wz.at[z, c], pair[h])
    send(wt.at[:, other], W.at[z, y, rows2, :], s_wz.at[7, 0], r_wz.at[z, c], partner)
    send(hid.at[:, other], H.at[c], s_d2d.at[0], r_d2d.at[0], partner)

    def wslab(yy, xx):
        return W.at[:, yy, pl.ds(4 * xx, 4), :]

    def whalf(yy, xx, h):
        return W.at[pl.ds(4 * h, 4), yy, pl.ds(4 * xx, 4), :]

    for zz in range(8):
        for cs in range(2):
            arrive(W.at[zz, y, pl.ds(4 * x + 2 * cs, 2), :], r_wz.at[zz, cs])
    for k in (1, 3, 2):
        send(wslab(y, x), wslab(y, x), s_wf.at[k - 1], r_w.at[y, x], F[k])

    for i in range(2):
        arrive(Gr.at[i], r_g.at[0, i])
        arrive(Gbr.at[i], r_g.at[1, i])
    send(Gr.at[0, 0:8], Gr.at[2, 0:8], s_g2.at[0], r_g2.at[0], up)
    send(Gr.at[1, 8:16], Gr.at[2, 8:16], s_g2.at[1], r_g2.at[1], down)
    send(Gbr.at[0], Gbr.at[2], s_g2.at[2], r_g2.at[2], up)

    for k in range(4):
        yy, xx = at_f(k)
        if k:
            arrive(wslab(yy, xx), r_w.at[yy, xx])
        for i, s in enumerate((1, 3)):
            send(wslab(yy, xx), wslab(yy, xx), s_ws.at[k, i], r_w.at[yy, xx], S[s])

    for l in loads[:5]:
        l.wait()
    arrive(Gr.at[2, 0:8], r_g2.at[0])
    arrive(Gr.at[2, 8:16], r_g2.at[1])
    arrive(Gbr.at[2], r_g2.at[2])
    scale = step_size / 4
    na[...] = (aav[...] - scale * ((gav[...] + Gr[0]) + (Gr[1] + Gr[2]))).astype(bf16)
    newb = abv[...] - scale * ((gbv[...] + Gbr[0]) + (Gbr[1] + Gbr[2]))
    nb[...] = newb
    adst = A.at[zs, y, x, pl.ds(16 * c, 16), :]
    bdst = B.at[z, y, x, pl.ds(2 * c, 2), :]
    for j, p in enumerate(zpeers):
        to = p[:4] + (zh,)
        send(na, adst, s_az.at[j], r_az.at[zs, c], to)
        send(nb, bdst, s_bz.at[j], r_bz.at[zs, c], to)
    own_a = pltpu.make_async_copy(na, adst, r_az.at[zs, c])
    own_b = pltpu.make_async_copy(nb, bdst, r_bz.at[zs, c])
    give_a = pltpu.make_async_remote_copy(na, adst, s_own.at[0], r_az.at[zs, c], partner, MESH)
    give_b = pltpu.make_async_remote_copy(nb, bdst, s_own.at[1], r_bz.at[zs, c], partner, MESH)

    @pl.when(zh == c)
    def _():
        own_a.start()
        own_b.start()

    @pl.when(zh != c)
    def _():
        give_a.start()
        give_b.start()

    send(nb, nbp, s_d2d.at[1], r_d2d.at[1], partner)

    fabs = x * oc + y * c
    for k in range(4):
        for i, (s, to) in enumerate(((3, 1), (1, 3))):
            yy, xx = at_f(k, s)
            arrive(wslab(yy, xx), r_w.at[yy, xx])
            send(whalf(yy, xx, i), whalf(yy, xx, i), s_w2.at[k, i], r_w2.at[lax.rem(fabs + k, 4), i], S[to])

    bz = pl.ds(4 * c, 4)
    for q in range(4):
        for cs in range(2):
            arrive(A.at[q, y, x, pl.ds(16 * cs, 16), :], r_az.at[q, cs])
            arrive(B.at[4 * c + q, y, x, pl.ds(2 * cs, 2), :], r_bz.at[q, cs])
    for k in (1, 3, 2):
        send(A.at[:, y, x], A.at[:, y, x], s_af.at[k - 1], r_a.at[y, x], F[k])
        send(B.at[bz, y, x], B.at[bz, y, x], s_bf.at[k - 1], r_b.at[y, x], F[k])
    for k in (0, 1, 3, 2):
        yy, xx = at_f(k)
        if k:
            arrive(A.at[:, yy, xx], r_a.at[yy, xx])
            arrive(B.at[bz, yy, xx], r_b.at[yy, xx])
        for s in (1, 3, 2):
            send(A.at[:, yy, xx], A.at[:, yy, xx], s_as.at[k, s - 1], r_a.at[yy, xx], S[s])
            send(B.at[bz, yy, xx], B.at[bz, yy, xx], s_bs.at[k, s - 1], r_b.at[yy, xx], S[s])

    for k in range(4):
        for i in range(2):
            yy, xx = at_f(k, 2)
            arrive(whalf(yy, xx, i), r_w2.at[lax.rem(fabs + k, 4), i])
    arrive(H.at[oc], r_d2d.at[0])
    loads[5].wait()

    def project(t):
        def tile(n, carry):
            w = W[pl.ds(4 * n, 4)].reshape(256, 2048)
            Pb[t, :, pl.ds(pl.multiple_of(n * 256, 256), 256)] = dot_nt(H[t], w)
            return carry

        lax.fori_loop(0, 2, tile, 0)

    project(oc)
    send(Pb.at[oc], Pin, s_d2d.at[2], r_d2d.at[2], partner)
    project(c)

    for k in range(4):
        for s in (1, 3, 2):
            yy, xx = at_f(k, s)
            arrive(B.at[bz, yy, xx], r_b.at[yy, xx])
    send(B.at[bz], B.at[bz], s_d2d.at[3], r_d2d.at[3], partner)
    for k in range(4):
        for s in (1, 3, 2):
            yy, xx = at_f(k, s)
            arrive(A.at[:, yy, xx], r_a.at[yy, xx])
    full_a = A[...].reshape(2048, 128)
    U[oc] = jnp.dot(H[oc], full_a, preferred_element_type=f32)
    send(U.at[oc], Uin, s_d2d.at[4], r_d2d.at[4], partner)

    arrive(nbp, r_d2d.at[1])
    hi, lo = split(newb)
    BL[0:2, :] = hi.astype(f32)
    BL[4:6, :] = lo.astype(f32)
    hi, lo = split(nbp[...])
    BL[2:4, :] = hi.astype(f32)
    BL[6:8, :] = lo.astype(f32)
    delta = dot_nt(BL[...].astype(bf16), full_a)
    D[...] = delta[2:4, :] + delta[6:8, :]
    send(D, Din, s_d2d.at[5], r_d2d.at[5], partner)
    mrg[:, mine] = (wv[:, mine].astype(f32) + (delta[0:2, :] + delta[4:6, :])).astype(bf16)

    U[c] = jnp.dot(H[c], full_a, preferred_element_type=f32)
    arrive(B.at[pl.ds(4 * oc, 4)], r_d2d.at[3])
    hi, lo = split(B.reshape(512, 128)[...])
    Bh[...] = hi
    Bl[...] = lo
    arrive(Pin, r_d2d.at[2])
    arrive(Uin, r_d2d.at[4])
    uh, ul = split(U[c] + Uin[...])
    acc = Pb[c] + Pin[...]
    acc = acc + (dot_nt(uh, Bh[...]) + (dot_nt(uh, Bl[...]) + dot_nt(ul, Bh[...])))
    out[...] = acc.astype(bf16)
    arrive(Din, r_d2d.at[5])
    mrg[:, other] = (wv[:, other].astype(f32) + Din[...]).astype(bf16)

    for d in pending:
        d.wait_send()

    @pl.when(zh != c)
    def _():
        give_a.wait_send()
        give_b.wait_send()


def shards(hidden, weight, adapter_a, adapter_b, grad_a, grad_b):
    V, sem = pltpu.VMEM, pltpu.SemaphoreType.DMA
    scratch = [
        V((2, 256, 2048), bf16),
        V((8, 4, 16, 2048), bf16),
        V((2, 256, 512), f32),
        V((256, 512), f32),
        V((2, 256, 128), f32),
        V((256, 128), f32),
        V((4, 4, 4, 32, 128), bf16),
        V((8, 4, 4, 4, 128), f32),
        V((512, 128), bf16),
        V((512, 128), bf16),
        V((16, 128), f32),
        V((2, 128), f32),
        V((16, 128), f32),
        V((2, 128), f32),
        V((3, 16, 128), f32),
        V((3, 2, 128), f32),
        V((16, 128), bf16),
        V((2, 128), f32),
        V((2, 128), f32),
        V((8, 128), f32),
        V((2, 2048), f32),
        V((2, 2048), f32),
        V((2, 4096), bf16),
        sem((6,)), sem((2,)), sem((2, 2)), sem((2, 2)), sem((3,)), sem((3,)),
        sem((8, 2)), sem((8, 2)), sem((3,)), sem((4, 4)), sem((4, 2)), sem((4, 2)), sem((4, 2)),
        sem((7,)), sem((4, 2)), sem((7,)), sem((4, 2)),
        sem((3,)), sem((4, 3)), sem((4, 4)), sem((3,)), sem((4, 3)), sem((4, 4)),
        sem((6,)), sem((6,)),
    ]
    hbm = pl.BlockSpec(memory_space=pltpu.HBM)
    vmem = pl.BlockSpec(memory_space=pltpu.VMEM)
    return pl.pallas_call(
        kernel,
        out_shape=(
            jax.ShapeDtypeStruct((256, 512), bf16),
            jax.ShapeDtypeStruct((2, 4096), bf16),
        ),
        in_specs=[hbm] * 6,
        out_specs=(vmem, vmem),
        scratch_shapes=scratch,
        compiler_params=pltpu.CompilerParams(
            collective_id=0, has_side_effects=True, vmem_limit_bytes=40 * 2**20
        ),
    )(*(pltpu.with_memory_space_constraint(a, pltpu.HBM) for a in (hidden, weight, adapter_a, adapter_b, grad_a, grad_b)))


def solution(mesh):
    finer = Mesh(
        mesh.devices.reshape(mesh.shape["rep"], 8, 4, 4, 2),
        ("rep", "fsdp_0", "fsdp_1", "fsdp_2", "fsdp_3"),
    )
    in_specs = (
        P(REP_FSDP, None),
        P(FSDP, None),
        P(FSDP, None),
        P(FSDP, None),
        P("rep", FSDP, None),
        P("rep", FSDP, None),
    )
    out_specs = (P(REP_FSDP, None), P(FSDP, None))
    return jax.shard_map(
        shards, mesh=finer, in_specs=in_specs, out_specs=out_specs, check_vma=False
    )
```
